256 devices in a mesh: gr: 32 (over x, y, core), gc: 8 (over z).
Axes of the slice: x: 4, y: 4, z: 8, core: 2. Of those that a mesh axis runs over, the one named last changes fastest.
Arguments:
- x_states: bfloat16 [262144, 512], P(('gr', 'gc'))
- y_states: bfloat16 [262144, 512], P(('gr', 'gc')), as said below
Outputs:
- proj_x: bfloat16 [262144, 512], P(('gr', 'gc'))
- proj_y: bfloat16 [262144, 512], P(('gr', 'gc'))
- cross: float32 [512, 512], replicated
Inputs may be any that keep to these rules, and one draw needn't show every extreme that they name: `y_states`: paired with x_states row by row.
All inputs are finite; a program needn't handle non-finite values.
Results may differ from the reference program's by a relative error of at most 0.0015.
Values sent between devices are 32-bit elements; how exact they have to be, the bound alone decides.
A program may use at most 64 MiB of HBM per device.

```python
import jax
import jax.numpy as jnp
from jax import lax

PW = 512
ROWS = 262144


def paired_states(key):
    base_key = jax.random.fold_in(key, 7001)
    k_one, k_two, k_three, k_four = jax.random.split(base_key, 4)
    source = jax.random.normal(k_one, (ROWS, PW), jnp.float32)
    noise = jax.random.normal(k_two, (ROWS, PW), jnp.float32)
    scale_x = jnp.exp(jax.random.uniform(k_three, (1, PW), jnp.float32, -1.2, 1.2))
    scale_y = jnp.exp(jax.random.uniform(k_four, (1, PW), jnp.float32, -1.2, 1.2))
    mixed = 0.5 * source + 0.4 * jnp.roll(source, 1, axis=1) + 0.3 * jnp.roll(source, -5, axis=1) + 0.3 * jnp.roll(source, 11, axis=1)
    x_full = source * scale_x
    y_full = (mixed + 0.6 * noise) * scale_y
    return (x_full, y_full)


def draw_x_states(key, part):
    return paired_states(key)[0].astype(jnp.bfloat16)


def draw_y_states(key, part):
    return paired_states(key)[1].astype(jnp.bfloat16)


def setup_inputs(seed: int = 0) -> dict:
    arg_keys = jax.random.split(jax.random.key(seed), 3)
    x_states = draw_x_states(jax.random.fold_in(arg_keys[2], 71), 0)
    y_states = draw_y_states(jax.random.fold_in(arg_keys[2], 71), 0)
    return {"x_states": x_states, "y_states": y_states}


RIDGE = 0.1

def reference(x_states, y_states):
    eye = jnp.eye(PW, dtype=jnp.float32)
    cov_x = jnp.dot(x_states.T.astype(jnp.float32), x_states.astype(jnp.float32), preferred_element_type=jnp.float32) / ROWS + RIDGE * eye
    cov_y = jnp.dot(y_states.T.astype(jnp.float32), y_states.astype(jnp.float32), preferred_element_type=jnp.float32) / ROWS + RIDGE * eye
    cov_xy = jnp.dot(x_states.T.astype(jnp.float32), y_states.astype(jnp.float32), preferred_element_type=jnp.float32) / ROWS
    low_x = jnp.linalg.cholesky(cov_x)
    low_y = jnp.linalg.cholesky(cov_y)
    left = jax.scipy.linalg.solve_triangular(low_x, cov_xy, lower=True)
    cross = jax.scipy.linalg.solve_triangular(low_y, left.T, lower=True).T
    white_x = jax.scipy.linalg.solve_triangular(low_x, x_states.astype(jnp.float32).T, lower=True).T
    white_y = jax.scipy.linalg.solve_triangular(low_y, y_states.astype(jnp.float32).T, lower=True).T
    proj_x = jnp.dot(white_x, cross, precision=lax.Precision.HIGHEST).astype(jnp.bfloat16)
    proj_y = jnp.dot(white_y, cross.T, precision=lax.Precision.HIGHEST).astype(jnp.bfloat16)
    return (proj_x, proj_y, cross)
```

```python
import jax
import jax.numpy as jnp
from jax import lax
from jax.experimental import pallas as pl
from jax.experimental.pallas import tpu as pltpu
from jax.sharding import PartitionSpec as P

RIDGE = 0.1
B = 128
NB = 4
HALF = 18 * B
UPPER = [(i, j) for i in range(NB) for j in range(i, NB)]
BLOCK_X = {ij: n for n, ij in enumerate(UPPER)}
BLOCK_Y = {ij: 18 + n for n, ij in enumerate(UPPER)}
BLOCK_XY = {(i, j): (10 if i < 2 else 24) + NB * i + j - (0 if i < 2 else 4) for i in range(NB) for j in range(NB)}
MESH = pl.DeviceIdType.MESH
PARTS = ((0, 1024, "xyz"), (1024, 1024, "yxz"), (2048, 256, "zxy"))
SIZE = {"x": 4, "y": 4, "z": 8}


def reduce_kernel(x_ref, y_ref, out_ref, acc, res, rc, r11, r12, r13, r21, r22, r23, r31, r32, r33,
                  s11, s12, s21, s22, s31, send_sem, recv_sem, out_sem):
    gr = lax.axis_index("gr")
    gc = lax.axis_index("gc")
    core = lax.rem(gr, 2)
    place = {"x": gr // 8, "y": lax.rem(gr // 2, 4), "z": gc}

    def peer(axis, d):
        to = lax.rem(place[axis] + d, SIZE[axis])
        p = dict(place)
        p[axis] = to
        return to, ((p["x"] * 4 + p["y"]) * 2 + core, p["z"])

    partner = (gr + 1 - 2 * core, gc)
    barrier = pltpu.get_barrier_semaphore()
    pl.semaphore_signal(barrier, inc=1, device_id=partner, device_id_type=MESH)
    for axis in "xyz":
        for d in range(1, SIZE[axis]):
            pl.semaphore_signal(barrier, inc=1, device_id=peer(axis, d)[1], device_id_type=MESH)

    def gram(a_ref, b_ref, i, first, index):
        g = lax.dot_general(a_ref[:, i * B : i * B + B], b_ref[:, first * B :], (((0,), (0,)), ((), ())),
                            preferred_element_type=jnp.float32)
        for j in range(first, NB):
            n = index[i, j]
            acc[n * B : n * B + B, :] = g[:, (j - first) * B : (j - first) * B + B]

    for i in range(NB):
        gram(x_ref, x_ref, i, i, BLOCK_X)
        gram(y_ref, y_ref, i, i, BLOCK_Y)
        gram(x_ref, y_ref, i, 0, BLOCK_XY)

    pl.semaphore_wait(barrier, 14)

    count = [0]

    def send(src, dst, to):
        k = count[0]
        count[0] += 1
        copy = pltpu.make_async_remote_copy(src_ref=src, dst_ref=dst, send_sem=send_sem.at[k], recv_sem=recv_sem.at[k],
                                            device_id=to, device_id_type=MESH)
        copy.start()
        return copy

    def rows(start, size):
        return pl.ds(pl.multiple_of(start, 8), size)

    mine = core * HALF
    c = send(acc.at[rows((1 - core) * HALF, HALF)], rc, partner)
    c.wait()
    rc[...] = rc[...] + acc[rows(mine, HALF), :]

    def scatter(src, base, size, axis, recv):
        copies = []
        for d in range(1, SIZE[axis]):
            to, dev = peer(axis, d)
            copies.append(send(src.at[rows(base + to * size, size)], recv.at[d - 1], dev))
        return copies

    def total(copies, src, base, size, axis, recv):
        for c in copies:
            c.wait()
        t = src[rows(base + place[axis] * size, size), :]
        for d in range(SIZE[axis] - 1):
            t = t + recv[d]
        return t

    def gather(pos, size, axis):
        at = res.at[rows(mine + pos, size)]
        return [send(at, at, peer(axis, d)[1]) for d in range(1, SIZE[axis])]

    x, y, z = place["x"], place["y"], place["z"]
    c1 = scatter(rc, 0, 256, "x", r11)
    c2 = scatter(rc, 1024, 256, "y", r21)
    c3 = scatter(rc, 2048, 32, "z", r31)
    s31[...] = total(c3, rc, 2048, 32, "z", r31)
    c3 = scatter(s31, 0, 8, "x", r32)
    s11[...] = total(c1, rc, 0, 256, "x", r11)
    c1 = scatter(s11, 0, 64, "y", r12)
    s21[...] = total(c2, rc, 1024, 256, "y", r21)
    c2 = scatter(s21, 0, 64, "x", r22)
    r33[rows(y * 8, 8), :] = total(c3, s31, 0, 8, "x", r32)
    at = r33.at[rows(y * 8, 8)]
    c3 = [send(at, at, peer("y", d)[1]) for d in range(1, 4)]
    s12[...] = total(c1, s11, 0, 64, "y", r12)
    c1 = scatter(s12, 0, 8, "z", r13)
    s22[...] = total(c2, s21, 0, 64, "x", r22)
    c2 = scatter(s22, 0, 8, "z", r23)
    for c in c3:
        c.wait()
    pos3 = 2048 + z * 32
    res[rows(mine + pos3 + x * 8, 8), :] = (r33[0:8, :] + r33[8:16, :]) + (r33[16:24, :] + r33[24:32, :])
    c3 = gather(pos3 + x * 8, 8, "x")
    pos1 = x * 256
    pos2 = 1024 + y * 256
    res[rows(mine + pos1 + y * 64 + z * 8, 8), :] = total(c1, s12, 0, 8, "z", r13)
    c1 = gather(pos1 + y * 64 + z * 8, 8, "z")
    res[rows(mine + pos2 + x * 64 + z * 8, 8), :] = total(c2, s22, 0, 8, "z", r23)
    c2 = gather(pos2 + x * 64 + z * 8, 8, "z")
    for c in c3:
        c.wait()
    c3 = gather(pos3, 32, "z")
    for c in c1:
        c.wait()
    c1 = gather(pos1 + y * 64, 64, "y")
    for c in c2:
        c.wait()
    c2 = gather(pos2 + x * 64, 64, "x")
    for c in c1:
        c.wait()
    c1 = gather(pos1, 256, "x")
    for c in c2:
        c.wait()
    c2 = gather(pos2, 256, "y")
    last = []
    for n, (copies, (first, size, _)) in enumerate(((c3, PARTS[2]), (c1, PARTS[0]), (c2, PARTS[1]))):
        for c in copies:
            c.wait()
        own = rows(mine + first, size)
        last.append(send(res.at[own], res.at[own], partner))
    for c in last:
        c.wait()
    o = pltpu.make_async_copy(res, out_ref, out_sem)
    o.start()
    o.wait()


N_COPIES = 1 + 2 * (3 + 3 + 7) * 2 + (7 + 3 + 3 + 3 + 7) + 3


def dot(a, b, dims=((1,), (0,))):
    return lax.dot_general(a, b, (dims, ((), ())), precision=lax.Precision.HIGHEST, preferred_element_type=jnp.float32)


def eliminate_rows(a_rows, g, lane, sub):
    c0 = 8 * g
    here = a_rows[g]
    n = len(a_rows)
    cols = [[jnp.broadcast_to(a_rows[t][:, c0 + j : c0 + j + 1], (8, B)) for j in range(8)] for t in range(g, n)]
    a = {(i, j): jnp.broadcast_to(cols[0][j][i : i + 1, :], (8, B)) for j in range(8) for i in range(j, 8)}
    low = {}
    inv = []
    for k in range(8):
        r = 1.0 / a[k, k]
        inv.append(r)
        for i in range(k + 1, 8):
            low[i, k] = a[i, k] * r
        for j in range(k + 1, 8):
            for i in range(j, 8):
                a[i, j] = a[i, j] - low[i, k] * a[j, k]
    in_group = (lane >= c0) & (lane < c0 + 8)
    here = jnp.where(in_group, jnp.where(lane - c0 == sub, 1.0, 0.0), here)
    up = []
    for k in range(8):
        u = jnp.broadcast_to(here[k : k + 1, :], (8, B))
        for j in range(k):
            u = u - low[k, j] * up[j]
        up.append(u)
    solved = [None] * 8
    for k in reversed(range(8)):
        s = up[k] * inv[k]
        for i in range(k + 1, 8):
            s = s - low[i, k] * solved[i]
        solved[k] = s
    out = list(a_rows)
    for t in range(g + 1, n):
        new = jnp.where(in_group, 0.0, a_rows[t])
        for j in range(8):
            new = new - cols[t - g][j] * solved[j]
        out[t] = new
    scaled = up[0] * lax.rsqrt(a[0, 0])
    for k in range(1, 8):
        scaled = jnp.where(sub == k, up[k] * lax.rsqrt(a[k, k]), scaled)
    out[g] = scaled
    return out


def invert_factors(mats):
    lane = lax.broadcasted_iota(jnp.int32, (8, B), 1)
    sub = lax.broadcasted_iota(jnp.int32, (8, B), 0)
    lower = lax.broadcasted_iota(jnp.int32, (B, B), 0) >= lax.broadcasted_iota(jnp.int32, (B, B), 1)
    for p in range(NB):
        blocks = [[m[p, p * B + 8 * t : p * B + 8 * t + 8, :] for t in range(16)] for m in mats]
        for g in range(16):
            blocks = [eliminate_rows(b, g, lane, sub) for b in blocks]
        for m, b in zip(mats, blocks):
            v = jnp.where(lower, jnp.concatenate(b, axis=0), 0.0)
            panel = []
            for c in range(NB):
                panel.append(v if c == p else dot(v, m[c, p * B : p * B + B, :]))
                m[c, p * B : p * B + B, :] = panel[c]
            for i in range(p + 1, NB):
                for c in list(range(p + 1)) + list(range(i, NB)):
                    u = dot(panel[i], panel[c], ((0,), (0,)))
                    m[c, i * B : i * B + B, :] = -u if c == p else m[c, i * B : i * B + B, :] - u


def project_kernel(total_rows, sums_ref, x_ref, y_ref, px_ref, py_ref, cross_ref, mx, my, low_x, low_y, work):
    def block(n):
        return sums_ref[n * B : n * B + B, :] / total_rows

    ridge = jnp.where(
        lax.broadcasted_iota(jnp.int32, (B, B), 0) == lax.broadcasted_iota(jnp.int32, (B, B), 1), RIDGE, 0.0
    )
    for i, j in UPPER:
        for m, index in ((mx, BLOCK_X), (my, BLOCK_Y)):
            b = block(index[i, j])
            m[j, i * B : i * B + B, :] = b + ridge if i == j else b
    invert_factors([mx, my])
    for m, low in ((mx, low_x), (my, low_y)):
        for i in range(NB):
            for c in range(i + 1):
                low[i * B : i * B + B, c * B : c * B + B] = m[c, i * B : i * B + B, :]
    cov_xy = [jnp.concatenate([block(BLOCK_XY[i, j]) for j in range(NB)], axis=1) for i in range(NB)]
    for i in range(NB):
        k = (i + 1) * B
        work[i * B : k, :] = dot(low_x[i * B : k, :k], jnp.concatenate(cov_xy[: i + 1], axis=0))
    for j in range(NB):
        k = (j + 1) * B
        cross_ref[:, j * B : k] = dot(work[:, :k], low_y[j * B : k, :k], ((1,), (1,)))
    for i in range(NB):
        work[i * B : i * B + B, :] = dot(low_x[i * B :, i * B : i * B + B], cross_ref[i * B :, :], ((0,), (0,)))
    for (z_ref, p_ref, dims) in ((x_ref, px_ref, ((1,), (0,))), (y_ref, py_ref, ((1,), (1,)))):
        if z_ref is y_ref:
            for j in range(NB):
                work[:, j * B : j * B + B] = dot(cross_ref[:, j * B :], low_y[j * B :, j * B : j * B + B])
        w = work[...]
        high = w.astype(jnp.bfloat16)
        rest = (w - high.astype(jnp.float32)).astype(jnp.bfloat16)
        z = z_ref[...]
        total = lax.dot_general(z, high, (dims, ((), ())), preferred_element_type=jnp.float32)
        total = total + lax.dot_general(z, rest, (dims, ((), ())), preferred_element_type=jnp.float32)
        p_ref[...] = total.astype(jnp.bfloat16)


def on_device(x_states, y_states):
    rows, width = x_states.shape
    total_rows = rows * lax.axis_size("gr") * lax.axis_size("gc")
    f32 = jnp.float32
    vmem = pl.BlockSpec(memory_space=pltpu.VMEM)

    def buf(*shape):
        return pltpu.VMEM(shape + (B,), f32)

    sums = pl.pallas_call(
        reduce_kernel,
        name="gram_reduce",
        out_shape=jax.ShapeDtypeStruct((2 * HALF, B), f32),
        in_specs=[vmem, vmem],
        out_specs=pl.BlockSpec(memory_space=pl.ANY),
        scratch_shapes=[
            buf(2 * HALF), buf(2 * HALF), buf(HALF),
            buf(3, 256), buf(3, 64), buf(7, 8), buf(3, 256), buf(3, 64), buf(7, 8), buf(7, 32), buf(3, 8), buf(32),
            buf(256), buf(64), buf(256), buf(64), buf(32),
            pltpu.SemaphoreType.DMA((N_COPIES,)), pltpu.SemaphoreType.DMA((N_COPIES,)), pltpu.SemaphoreType.DMA,
        ],
        compiler_params=pltpu.CompilerParams(collective_id=0, has_side_effects=True, vmem_limit_bytes=48 << 20),
    )(x_states, y_states)
    bf16 = jnp.bfloat16

    def project(sums_ref, *refs):
        project_kernel(float(total_rows), sums_ref, *refs)

    return pl.pallas_call(
        project,
        name="factor_project",
        out_shape=(
            jax.ShapeDtypeStruct((rows, width), bf16),
            jax.ShapeDtypeStruct((rows, width), bf16),
            jax.ShapeDtypeStruct((width, width), f32),
        ),
        in_specs=[vmem, vmem, vmem],
        out_specs=(vmem, vmem, vmem),
        scratch_shapes=[buf(NB, width), buf(NB, width)] + [pltpu.VMEM((width, width), f32)] * 3,
        compiler_params=pltpu.CompilerParams(vmem_limit_bytes=48 << 20),
    )(sums, x_states, y_states)


def solution(mesh):
    return jax.shard_map(
        on_device,
        mesh=mesh,
        in_specs=(P(("gr", "gc"), None), P(("gr", "gc"), None)),
        out_specs=(P(("gr", "gc"), None), P(("gr", "gc"), None), P()),
        check_vma=False,
    )
```

```python
import jax
import jax.numpy as jnp
from jax import lax
from jax.experimental import pallas as pl
from jax.experimental.pallas import tpu as pltpu
from jax.sharding import PartitionSpec as P

RIDGE = 0.1
F32 = jnp.float32
BF16 = jnp.bfloat16
B = 128
NB = 4
HALF = 18 * B
UPPER = [(i, j) for i in range(NB) for j in range(i, NB)]
BLOCK_X = {ij: n for n, ij in enumerate(UPPER)}
BLOCK_Y = {ij: 18 + n for n, ij in enumerate(UPPER)}
BLOCK_XY = {(i, j): (10 if i < 2 else 24) + NB * i + j - (0 if i < 2 else 4) for i in range(NB) for j in range(NB)}
MESH = pl.DeviceIdType.MESH
PARTS = ((0, 1024, "xyz"), (1024, 1024, "yxz"), (2048, 256, "zxy"))
SIZE = {"x": 4, "y": 4, "z": 8}


def reduce_kernel(x_ref, y_ref, out_ref, acc, res, rc, r11, r12, r13, r21, r22, r23, r31, r32, r33,
                  s11, s12, s21, s22, s31, send_sem, recv_sem, out_sem):
    gr = lax.axis_index("gr")
    gc = lax.axis_index("gc")
    core = lax.rem(gr, 2)
    place = {"x": gr // 8, "y": lax.rem(gr // 2, 4), "z": gc}

    def peer(axis, d):
        to = lax.rem(place[axis] + d, SIZE[axis])
        p = dict(place)
        p[axis] = to
        return to, ((p["x"] * 4 + p["y"]) * 2 + core, p["z"])

    partner = (gr + 1 - 2 * core, gc)
    barrier = pltpu.get_barrier_semaphore()
    pl.semaphore_signal(barrier, inc=1, device_id=partner, device_id_type=MESH)
    for axis in "xyz":
        for d in range(1, SIZE[axis]):
            pl.semaphore_signal(barrier, inc=1, device_id=peer(axis, d)[1], device_id_type=MESH)

    def gram(a_ref, b_ref, i, first, index):
        g = lax.dot_general(a_ref[:, i * B : i * B + B], b_ref[:, first * B :], (((0,), (0,)), ((), ())),
                            preferred_element_type=jnp.float32)
        for j in range(first, NB):
            n = index[i, j]
            acc[n * B : n * B + B, :] = g[:, (j - first) * B : (j - first) * B + B]

    for i in range(NB):
        gram(x_ref, x_ref, i, i, BLOCK_X)
        gram(y_ref, y_ref, i, i, BLOCK_Y)
        gram(x_ref, y_ref, i, 0, BLOCK_XY)

    pl.semaphore_wait(barrier, 14)

    count = [0]

    def send(src, dst, to):
        k = count[0]
        count[0] += 1
        copy = pltpu.make_async_remote_copy(src_ref=src, dst_ref=dst, send_sem=send_sem.at[k], recv_sem=recv_sem.at[k],
                                            device_id=to, device_id_type=MESH)
        copy.start()
        return copy

    def rows(start, size):
        return pl.ds(pl.multiple_of(start, 8), size)

    mine = core * HALF
    c = send(acc.at[rows((1 - core) * HALF, HALF)], rc, partner)
    c.wait()
    rc[...] = rc[...] + acc[rows(mine, HALF), :]

    def scatter(src, base, size, axis, recv):
        copies = []
        for d in range(1, SIZE[axis]):
            to, dev = peer(axis, d)
            copies.append(send(src.at[rows(base + to * size, size)], recv.at[d - 1], dev))
        return copies

    def total(copies, src, base, size, axis, recv):
        for c in copies:
            c.wait()
        t = src[rows(base + place[axis] * size, size), :]
        for d in range(SIZE[axis] - 1):
            t = t + recv[d]
        return t

    def gather(pos, size, axis):
        at = res.at[rows(mine + pos, size)]
        return [send(at, at, peer(axis, d)[1]) for d in range(1, SIZE[axis])]

    x, y, z = place["x"], place["y"], place["z"]
    c1 = scatter(rc, 0, 256, "x", r11)
    c2 = scatter(rc, 1024, 256, "y", r21)
    c3 = scatter(rc, 2048, 32, "z", r31)
    s31[...] = total(c3, rc, 2048, 32, "z", r31)
    c3 = scatter(s31, 0, 8, "x", r32)
    s11[...] = total(c1, rc, 0, 256, "x", r11)
    c1 = scatter(s11, 0, 64, "y", r12)
    s21[...] = total(c2, rc, 1024, 256, "y", r21)
    c2 = scatter(s21, 0, 64, "x", r22)
    r33[rows(y * 8, 8), :] = total(c3, s31, 0, 8, "x", r32)
    at = r33.at[rows(y * 8, 8)]
    c3 = [send(at, at, peer("y", d)[1]) for d in range(1, 4)]
    s12[...] = total(c1, s11, 0, 64, "y", r12)
    c1 = scatter(s12, 0, 8, "z", r13)
    s22[...] = total(c2, s21, 0, 64, "x", r22)
    c2 = scatter(s22, 0, 8, "z", r23)
    for c in c3:
        c.wait()
    pos3 = 2048 + z * 32
    res[rows(mine + pos3 + x * 8, 8), :] = (r33[0:8, :] + r33[8:16, :]) + (r33[16:24, :] + r33[24:32, :])
    c3 = gather(pos3 + x * 8, 8, "x")
    pos1 = x * 256
    pos2 = 1024 + y * 256
    res[rows(mine + pos1 + y * 64 + z * 8, 8), :] = total(c1, s12, 0, 8, "z", r13)
    c1 = gather(pos1 + y * 64 + z * 8, 8, "z")
    res[rows(mine + pos2 + x * 64 + z * 8, 8), :] = total(c2, s22, 0, 8, "z", r23)
    c2 = gather(pos2 + x * 64 + z * 8, 8, "z")
    for c in c3:
        c.wait()
    c3 = gather(pos3, 32, "z")
    for c in c1:
        c.wait()
    c1 = gather(pos1 + y * 64, 64, "y")
    for c in c2:
        c.wait()
    c2 = gather(pos2 + x * 64, 64, "x")
    for c in c1:
        c.wait()
    c1 = gather(pos1, 256, "x")
    for c in c2:
        c.wait()
    c2 = gather(pos2, 256, "y")
    last = []
    for n, (copies, (first, size, _)) in enumerate(((c3, PARTS[2]), (c1, PARTS[0]), (c2, PARTS[1]))):
        for c in copies:
            c.wait()
        own = rows(mine + first, size)
        last.append(send(res.at[own], res.at[own], partner))
    for c in last:
        c.wait()
    o = pltpu.make_async_copy(res, out_ref, out_sem)
    o.start()
    o.wait()


N_COPIES = 1 + 2 * (3 + 3 + 7) * 2 + (7 + 3 + 3 + 3 + 7) + 3


def split3(a):
    a1 = a.astype(BF16)
    r = a - a1.astype(F32)
    a2 = r.astype(BF16)
    return a1, a2, (r - a2.astype(F32)).astype(BF16)


def dot_terms(a, b, pairs, dims):
    left = jnp.concatenate([a[m] for m, _ in pairs], axis=dims[0])
    right = jnp.concatenate([b[n] for _, n in pairs], axis=dims[1])
    return lax.dot_general(left, right, (((dims[0],), (dims[1],)), ((), ())), preferred_element_type=F32)


def dot6(a, b, dims=(1, 0)):
    return dot_terms(a, b, ((0, 0), (0, 1), (1, 0), (1, 1), (0, 2), (2, 0)), dims)


def dot3(a, b, dims=(1, 0)):
    return dot_terms(a, b, ((0, 0), (0, 1), (1, 0)), dims)


def eliminate_rows(a_rows, g, lane, sub):
    c0 = 8 * g
    here = a_rows[g]
    n = len(a_rows)
    cols = [[jnp.broadcast_to(a_rows[t][:, c0 + j : c0 + j + 1], (8, B)) for t in range(g, n)] for j in range(8)]

    def row(v, i):
        return jnp.take_along_axis(v, jnp.full((8, B), i, jnp.int32), axis=0, mode="promise_in_bounds")

    a = {(i, j): row(cols[j][0], i) for j in range(8) for i in range(j, 8)}
    low = {}
    inv = []
    for k in range(8):
        r = 1.0 / a[k, k]
        inv.append(r)
        for i in range(k + 1, 8):
            low[i, k] = a[i, k] * r
        for j in range(k + 1, 8):
            for i in range(j, 8):
                a[i, j] = a[i, j] - low[i, k] * a[j, k]
    in_group = (lane >= c0) & (lane < c0 + 8)
    here = jnp.where(in_group, jnp.where(lane - c0 == sub, 1.0, 0.0), here)
    up = []
    for k in range(8):
        u = jnp.broadcast_to(here[k : k + 1, :], (8, B))
        for j in range(k):
            u = u - low[k, j] * up[j]
        up.append(u)
    solved = [None] * 8
    for k in reversed(range(8)):
        s = up[k] * inv[k]
        for i in range(k + 1, 8):
            s = s - low[i, k] * solved[i]
        solved[k] = s
    out = list(a_rows)
    for t in range(g + 1, n):
        new = jnp.where(in_group, 0.0, a_rows[t])
        for j in range(8):
            new = new - cols[j][t - g] * solved[j]
        out[t] = new
    scaled = up[0] * lax.rsqrt(a[0, 0])
    for k in range(1, 8):
        scaled = jnp.where(sub == k, up[k] * lax.rsqrt(a[k, k]), scaled)
    out[g] = scaled
    return out


class Panel:
    def __init__(self, m, p, v):
        self.m, self.p, self.rows = m, p, slice(p * B, p * B + B)
        m[p, self.rows, :] = v
        self.v = split3(v)
        self.parts = {p: self.v}
        self.turned = {}

    def solve(self, columns):
        z = dot6(self.v, split3(jnp.concatenate([self.m[c, self.rows, :] for c in columns], axis=1)))
        for n, c in enumerate(columns):
            zc = z[:, n * B : n * B + B]
            self.m[c, self.rows, :] = zc
            self.parts[c] = split3(zc)

    def update(self, i, columns):
        if i not in self.turned:
            self.turned[i] = tuple(s.T for s in self.parts[i])
        u = dot6(self.turned[i], tuple(jnp.concatenate([self.parts[c][k] for c in columns], axis=1) for k in range(3)))
        for n, c in enumerate(columns):
            uc = u[:, n * B : n * B + B]
            at = (c, slice(i * B, i * B + B))
            self.m[at] = -uc if c == self.p else self.m[at] - uc


def invert_factors(mats, pending, on_panel):
    lane = lax.broadcasted_iota(jnp.int32, (8, B), 1)
    sub = lax.broadcasted_iota(jnp.int32, (8, B), 0)
    lower = lax.broadcasted_iota(jnp.int32, (B, B), 0) >= lax.broadcasted_iota(jnp.int32, (B, B), 1)
    for p in range(NB):
        blocks = [[m[p, p * B + 8 * t : p * B + 8 * t + 8, :] for t in range(16)] for m in mats]
        per = -(-len(pending) // 15)
        for g in range(16):
            blocks = [eliminate_rows(b, g, lane, sub) for b in blocks]
            for _ in range(min(per, len(pending))):
                pending.pop(0)()
        panels = [Panel(m, p, jnp.where(lower, jnp.concatenate(b, axis=0), 0.0)) for m, b in zip(mats, blocks)]
        if p + 1 == NB:
            for q in panels:
                q.solve(list(range(p)))
        else:
            for q in panels:
                q.solve([p + 1])
            for q in panels:
                q.update(p + 1, [p + 1])
            for q in panels:
                pending.append(lambda q=q, cs=[c for c in range(NB) if c not in (p, p + 1)]: q.solve(cs))
            for i in range(p + 1, NB):
                cs = list(range(p + 1)) + [c for c in range(i, NB) if c != p + 1]
                for q in panels:
                    for h in range(0, len(cs), 2):
                        pending.append(lambda q=q, i=i, cs=cs[h : h + 2]: q.update(i, cs))
        pending.extend(on_panel(p))
    for f in pending:
        f()


def project_kernel(total_rows, sums_ref, x_ref, y_ref, px_ref, py_ref, cross_ref,
                   mx, my, work, cross, xy, low_x, low_y, px, py, sems):
    def block(n):
        return sums_ref[n * B : n * B + B, :] / total_rows

    def at(i):
        return slice(i * B, i * B + B)

    ridge = jnp.where(
        lax.broadcasted_iota(jnp.int32, (B, B), 0) == lax.broadcasted_iota(jnp.int32, (B, B), 1), RIDGE, 0.0
    )

    def load(i, j):
        for m, index in ((mx, BLOCK_X), (my, BLOCK_Y)):
            b = block(index[i, j])
            m[j, at(i), :] = b + ridge if i == j else b

    def split_xy(i):
        for k, s in enumerate(split3(jnp.concatenate([block(BLOCK_XY[i, j]) for j in range(NB)], axis=1))):
            xy[k, at(i), :] = s

    def keep(p):
        for m, low in ((mx, low_x), (my, low_y)):
            for c in range(p + 1):
                for k, s in enumerate(split3(m[c, at(p), :])):
                    low[k, at(p), at(c)] = s

    def pieces(ref, *index):
        return tuple(ref[(k,) + index] for k in range(ref.shape[0]))

    def left(p):
        upto = slice(0, p * B + B)
        for k, s in enumerate(split3(dot6(pieces(low_x, at(p), upto), pieces(xy, upto, slice(None))))):
            work[k, at(p), :] = s

    def cross_block(rows, j):
        upto = slice(0, j * B + B)
        t = dot6(pieces(work, rows, upto), pieces(low_y, at(j), upto), (1, 1))
        cross[rows, at(j)] = t

    def on_panel(p):
        jobs = [lambda: keep(p), lambda: left(p), lambda: cross_block(slice(0, p * B + B), p)]
        return jobs + [lambda j=j: cross_block(at(p), j) for j in range(p)]

    load(0, 0)
    rest = [ij for ij in UPPER if ij != (0, 0)]
    pending = [lambda ij=ij: load(*ij) for ij in rest] + [lambda i=i: split_xy(i) for i in range(NB)]
    invert_factors([mx, my], pending, on_panel)

    copies = [pltpu.make_async_copy(cross, cross_ref, sems.at[0])]
    copies[0].start()
    whole = cross[...]
    c1 = whole.astype(BF16)
    c2 = (whole - c1.astype(F32)).astype(BF16)

    def two(w):
        w1 = w.astype(BF16)
        return w1, (w - w1.astype(F32)).astype(BF16)

    for i in range(NB):
        k = slice(i * B, None)
        w = dot3((low_x[0, k, at(i)], low_x[1, k, at(i)]), (c1[k], c2[k]), (0, 0))
        work[0, at(i), :], work[1, at(i), :] = two(w)
    wx = jnp.concatenate([work[0], work[1]], axis=0)
    for h in range(2):
        r = slice(h * x_ref.shape[0] // 2, (h + 1) * x_ref.shape[0] // 2)
        x = x_ref[r, :]
        px[r, :] = jnp.dot(jnp.concatenate([x, x], axis=1), wx, preferred_element_type=F32).astype(BF16)
        copies.append(pltpu.make_async_copy(px.at[r, :], px_ref.at[r, :], sems.at[1 + h]))
        copies[-1].start()
    for j in range(NB):
        k = slice(j * B, None)
        w = dot3((c1[:, k], c2[:, k]), (low_y[0, k, at(j)], low_y[1, k, at(j)]))
        xy[0, :, at(j)], xy[1, :, at(j)] = two(w)
    wy = jnp.concatenate([xy[0], xy[1]], axis=1)
    for h in range(2):
        r = slice(h * y_ref.shape[0] // 2, (h + 1) * y_ref.shape[0] // 2)
        y = y_ref[r, :]
        t = lax.dot_general(jnp.concatenate([y, y], axis=1), wy, (((1,), (1,)), ((), ())), preferred_element_type=F32)
        py[r, :] = t.astype(BF16)
        copies.append(pltpu.make_async_copy(py.at[r, :], py_ref.at[r, :], sems.at[3 + h]))
        copies[-1].start()
    for c in copies:
        c.wait()


def on_device(x_states, y_states):
    rows, width = x_states.shape
    total_rows = rows * lax.axis_size("gr") * lax.axis_size("gc")
    vmem = pl.BlockSpec(memory_space=pltpu.VMEM)
    anywhere = pl.BlockSpec(memory_space=pl.ANY)

    def buf(*shape):
        return pltpu.VMEM(shape + (B,), F32)

    sums = pl.pallas_call(
        reduce_kernel,
        name="gram_reduce",
        out_shape=jax.ShapeDtypeStruct((2 * HALF, B), F32),
        in_specs=[vmem, vmem],
        out_specs=anywhere,
        scratch_shapes=[
            buf(2 * HALF), buf(2 * HALF), buf(HALF),
            buf(3, 256), buf(3, 64), buf(7, 8), buf(3, 256), buf(3, 64), buf(7, 8), buf(7, 32), buf(3, 8), buf(32),
            buf(256), buf(64), buf(256), buf(64), buf(32),
            pltpu.SemaphoreType.DMA((N_COPIES,)), pltpu.SemaphoreType.DMA((N_COPIES,)), pltpu.SemaphoreType.DMA,
        ],
        compiler_params=pltpu.CompilerParams(collective_id=0, has_side_effects=True, vmem_limit_bytes=48 << 20),
    )(x_states, y_states)

    def project(sums_ref, *refs):
        project_kernel(float(total_rows), sums_ref, *refs)

    return pl.pallas_call(
        project,
        name="factor_project",
        out_shape=(
            jax.ShapeDtypeStruct((rows, width), BF16),
            jax.ShapeDtypeStruct((rows, width), BF16),
            jax.ShapeDtypeStruct((width, width), F32),
        ),
        in_specs=[vmem, vmem, vmem],
        out_specs=(anywhere, anywhere, anywhere),
        scratch_shapes=[
            buf(NB, width), buf(NB, width),
            pltpu.VMEM((3, width, width), BF16), pltpu.VMEM((width, width), F32),
            pltpu.VMEM((3, width, width), BF16), pltpu.VMEM((3, width, width), BF16), pltpu.VMEM((3, width, width), BF16),
            pltpu.VMEM((rows, width), BF16), pltpu.VMEM((rows, width), BF16),
            pltpu.SemaphoreType.DMA((5,)),
        ],
        compiler_params=pltpu.CompilerParams(vmem_limit_bytes=48 << 20),
    )(sums, x_states, y_states)


def solution(mesh):
    return jax.shard_map(
        on_device,
        mesh=mesh,
        in_specs=(P(("gr", "gc"), None), P(("gr", "gc"), None)),
        out_specs=(P(("gr", "gc"), None), P(("gr", "gc"), None), P()),
        check_vma=False,
    )
```
